256 devices in a mesh: subj: 8 (over y_hi, x), cortex: 32 (over y_lo, z, core).
Axes of the slice: x: 4, y: 4 (y_hi: 2, y_lo: 2; y = y_hi * 2 + y_lo), z: 8, core: 2. Of those that a mesh axis runs over, the one named last changes fastest.
Arguments:
- series: bfloat16 [16, 1024, 8192], P('subj', None, 'cortex'), may hold values from -6 to 6
- template: bfloat16 [1024, 8192], P(None, 'cortex'), may hold values from -6 to 6
- sl_blocks: int32 [64, 3], P('cortex'), may hold values from 0 to 63, as said below
Outputs:
- template_new: float32 [1024, 8192], P(None, 'cortex')
The draws below stay inside these ranges and needn't reach their ends.
Inputs may be any that keep to these rules, and one draw needn't show every extreme that they name: sl_blocks[g, 0] = g; the other two entries of row g are distinct, differ from g, and lie between (g // 2 - 1) * 2 and (g // 2 + 2) * 2 - 1.
All inputs are finite; a program needn't handle non-finite values.
Results may differ from the reference program's by a relative error of at most 0.0024.
Values may be sent and summed in bfloat16 or wider, within the bound.
A program may use at most 64 MiB of HBM per device.

```python
import jax
import jax.numpy as jnp
from jax import lax

BLOCK = 128
NS_STEPS = 8
FRAMES = 1024
BLK_DEV = 2
SUBJECTS = 16
NBLOCKS = 64
VERTS = 8192


def draw_sl_blocks(key, part):
    first_key, second_key = jax.random.split(jax.random.fold_in(key, 7))
    centre = jnp.arange(NBLOCKS, dtype=jnp.int32)
    owner_dev = centre // BLK_DEV
    window_low = jnp.maximum((owner_dev - 1) * BLK_DEV, 0)
    window_high = jnp.minimum((owner_dev + 2) * BLK_DEV, NBLOCKS)
    span_size = window_high - window_low
    position = centre - window_low
    first_pick = jax.random.randint(first_key, (NBLOCKS,), 0, span_size - 1)
    first_pick = first_pick + (first_pick >= position).astype(jnp.int32)
    lower_mark = jnp.minimum(position, first_pick)
    upper_mark = jnp.maximum(position, first_pick)
    second_pick = jax.random.randint(second_key, (NBLOCKS,), 0, span_size - 2)
    second_pick = second_pick + (second_pick >= lower_mark).astype(jnp.int32)
    second_pick = second_pick + (second_pick >= upper_mark).astype(jnp.int32)
    return jnp.stack([centre, window_low + first_pick, window_low + second_pick], axis=1).astype(jnp.int32)


def shard_levels(key, dims, cuts, least, largest):
    def one(dim, parts):
        draws = jax.random.uniform(jax.random.fold_in(jax.random.fold_in(key, 6), dim), (parts,), jnp.float32, least / len(cuts), largest / len(cuts))
        return jnp.repeat(jnp.exp(draws), dims[dim] // parts).reshape((-1,) + (1,) * (len(dims) - dim - 1))

    gain = one(*cuts[0])
    for cut in cuts[1:]:
        gain = gain * one(*cut)
    return gain


def bell_draw(key, extent, spread, bound, cuts=(), kind=jnp.bfloat16):
    result = jax.random.normal(key, extent, jnp.float32) * spread
    if len(cuts) > 0:
        result = shard_levels(key, extent, cuts, -0.22, 0.18) * result
    return jnp.clip(result, min=-bound, max=bound).astype(kind)


def setup_inputs(seed: int = 0) -> dict:
    key_list = jax.random.split(jax.random.key(seed), 4)
    series = bell_draw(key_list[0], (SUBJECTS, FRAMES, VERTS), 1.0, 6.0, ((0, 8), (2, 32)))
    template = bell_draw(key_list[1], (FRAMES, VERTS), 1.0, 6.0, ((1, 32),))
    sl_blocks = draw_sl_blocks(jax.random.fold_in(key_list[3], 71), 0)
    return {"series": series, "template": template, "sl_blocks": sl_blocks}


RIDGE_SHIFT = 0.1
NORM_EPSILON = 1e-06

def rounded(value):
    return lax.optimization_barrier(value.astype(jnp.bfloat16))

def polar_factor(cross_prod):
    squares = lax.optimization_barrier(jnp.sum(cross_prod * cross_prod, axis=(1, 2), keepdims=True))
    current = rounded(cross_prod / jnp.sqrt(squares + NORM_EPSILON))
    for iteration in range(NS_STEPS):
        wide_map = current.astype(jnp.float32)
        gram_mat = rounded(jnp.einsum('sab,sac->sbc', wide_map, wide_map, precision=lax.Precision.HIGHEST))
        product = jnp.einsum('sab,sbc->sac', wide_map, gram_mat.astype(jnp.float32), precision=lax.Precision.HIGHEST)
        current = rounded(1.5 * wide_map - 0.5 * product)
    return current

def reference(series, template, sl_blocks):
    subj_count = series.shape[0]
    offsets = jnp.arange(BLOCK, dtype=jnp.int32)
    identity = jnp.eye(3 * BLOCK, dtype=jnp.float32)

    def visit_one(running, blocks):
        columns = (blocks[:, None] * BLOCK + offsets[None, :]).reshape(-1).astype(jnp.int32)
        subj_cols = jnp.take(series, columns, axis=2).astype(jnp.float32)
        tmpl_cols = jnp.take(template, columns, axis=1).astype(jnp.float32)
        cross_prod = jnp.einsum('sfa,fb->sab', subj_cols, tmpl_cols, precision=lax.Precision.HIGHEST) / FRAMES + RIDGE_SHIFT * identity
        polar_map = polar_factor(cross_prod)
        mapped = jnp.einsum('sfa,sab->sfb', subj_cols, polar_map.astype(jnp.float32), precision=lax.Precision.HIGHEST)
        running = running.at[:, columns].add(lax.optimization_barrier(jnp.sum(mapped, axis=0)))
        return (running, None)
    running = jnp.zeros((FRAMES, VERTS), jnp.float32)
    running, unused = lax.scan(visit_one, running, sl_blocks)
    block_ids = sl_blocks.reshape(-1)
    coverage = lax.optimization_barrier(jnp.sum((block_ids[:, None] == jnp.arange(NBLOCKS, dtype=jnp.int32)[None, :]).astype(jnp.float32), axis=0))
    per_vertex = jnp.repeat(coverage, BLOCK)
    return running / per_vertex[None, :] / subj_count
```

```python
import functools

import jax
import jax.numpy as jnp
from jax import lax
from jax.experimental import pallas as pl
from jax.experimental.pallas import tpu as pltpu
from jax.sharding import PartitionSpec as P

BLOCK = 128
NS_STEPS = 8
BLK_DEV = 2
SPAN = 3
WIN = 3 * BLK_DEV
RIDGE_SHIFT = 0.1
NORM_EPSILON = 1e-06
CHUNKS = 4
MESH = pl.DeviceIdType.MESH
LINK = jnp.bfloat16


def kernel(
    subj_devs, cortex_devs, lists, series, template, gathered,
    win_x0, win_x1, win_p, seen_x, seen_pt, maps, last_maps, tiles, own, back_out, back_in,
    part_out, part_in, mean_out, count_out, count_in,
    load_sem, halo_send, halo_recv, count_send, count_recv,
    back_send, back_recv, part_send, part_recv, mean_send, mean_recv,
):
    subjects, frames = series.shape[0], series.shape[1]
    width = SPAN * BLOCK
    rows = frames // CHUNKS
    piece = rows // subj_devs
    me_s, me_c = lax.axis_index("subj"), lax.axis_index("cortex")
    left = (me_s, lax.rem(me_c + cortex_devs - 1, cortex_devs))
    right = (me_s, lax.rem(me_c + 1, cortex_devs))
    sides = (left, right)
    win_x = (win_x0, win_x1)
    peers = [lax.rem(me_s + d, subj_devs) for d in range(subj_devs)]

    barrier = pltpu.get_barrier_semaphore()
    for device in (*sides, *((p, me_c) for p in peers[1:])):
        pl.semaphore_signal(barrier, inc=1, device_id=device, device_id_type=MESH)

    loads = []
    for b in range(BLK_DEV):
        cols = pl.ds(b * BLOCK, BLOCK)
        loads.append((template.at[:, cols], win_p.at[BLK_DEV + b]))
        for s in range(subjects):
            loads.append((series.at[s, :, cols], win_x[s].at[BLK_DEV + b]))
    loads = [pltpu.make_async_copy(a, b, load_sem.at[i]) for i, (a, b) in enumerate(loads)]
    for copy in loads:
        copy.start()

    first = (me_c - 1) * BLK_DEV
    place = [
        [jnp.clip(lists[g, a] - first, 0, WIN - 1) for a in range(SPAN)] for g in range(BLK_DEV)
    ]
    entry = [
        [
            jnp.where(p[0] == w, 0, jnp.where(p[1] == w, 1, jnp.where(p[2] == w, 2, SPAN)))
            for w in range(WIN)
        ]
        for p in place
    ]
    counts = []
    for w in range(WIN):
        c = sum(jnp.where(p == w, 1.0, 0.0) for q in place for p in q)
        counts.append(jnp.full((8, BLOCK), c, jnp.float32))
    for b in range(BLK_DEV):
        count_out[0, pl.ds(8 * b, 8)] = counts[b]
        count_out[1, pl.ds(8 * b, 8)] = counts[2 * BLK_DEV + b]
    for g in range(BLK_DEV):
        tiles[g, SPAN] = jnp.zeros(tiles.shape[2:], tiles.dtype)

    pl.semaphore_wait(barrier, 2 + subj_devs - 1)

    halo = {}
    for item in range(1 + subjects):
        for side in range(2):
            for b in range(BLK_DEV):
                cols = pl.ds(b * BLOCK, BLOCK)
                spot = (2 * BLK_DEV if side == 0 else 0) + b
                if item == 0:
                    src, dst = template.at[:, cols], win_p.at[spot]
                else:
                    src, dst = series.at[item - 1, :, cols], win_x[item - 1].at[spot]
                copy = pltpu.make_async_remote_copy(
                    src, dst, halo_send.at[item, side, b], halo_recv.at[item, side, b],
                    device_id=sides[side], device_id_type=MESH,
                )
                copy.start()
                halo[item, side, b] = copy
    tally = []
    for side in range(2):
        copy = pltpu.make_async_remote_copy(
            count_out.at[side], count_in.at[side], count_send.at[side], count_recv.at[side],
            device_id=sides[side], device_id_type=MESH,
        )
        copy.start()
        tally.append(copy)
    for copy in loads:
        copy.wait()

    def arrived(item):
        for side in range(2):
            for b in range(BLK_DEV):
                halo[item, side, b].wait_recv()

    on_diagonal = lax.broadcasted_iota(jnp.int32, (width, width), 0) == lax.broadcasted_iota(
        jnp.int32, (width, width), 1
    )
    arrived(0)
    for g in range(BLK_DEV):
        for a in range(SPAN):
            seen_pt[g, pl.ds(a * BLOCK, BLOCK), :] = win_p[place[g][a]].T
    for s in range(subjects):
        arrived(1 + s)
        for g in range(BLK_DEV):
            for a in range(SPAN):
                seen_x[g, :, pl.ds((s * SPAN + a) * BLOCK, BLOCK)] = win_x[s][place[g][a]]
        for g in range(BLK_DEV):
            cross = lax.dot_general(
                seen_pt[g], seen_x[g, :, pl.ds(s * width, width)], (((1,), (0,)), ((), ())),
                preferred_element_type=jnp.float32,
            )
            cross = cross * (1.0 / frames) + jnp.where(on_diagonal, RIDGE_SHIFT, 0.0)
            scale = lax.rsqrt(jnp.sum(cross * cross, keepdims=True) + NORM_EPSILON)
            maps[g] = (cross * scale).astype(jnp.bfloat16)

        def step(_, carry):
            for g in range(BLK_DEV):
                now = maps[g]
                gram = lax.dot_general(
                    now, now, (((1,), (1,)), ((), ())), preferred_element_type=jnp.float32
                ).astype(jnp.bfloat16)
                product = lax.dot_general(
                    gram, now, (((1,), (0,)), ((), ())), preferred_element_type=jnp.float32
                )
                maps[g] = (1.5 * now.astype(jnp.float32) - 0.5 * product).astype(jnp.bfloat16)
            return carry

        lax.fori_loop(0, NS_STEPS, step, 0)
        for g in range(BLK_DEV):
            last_maps[g, :, pl.ds(s * width, width)] = maps[g]

    for copy in tally:
        copy.wait()
    shares = []
    for b in range(BLK_DEV):
        total = counts[BLK_DEV + b] + count_in[0, pl.ds(8 * b, 8)] + count_in[1, pl.ds(8 * b, 8)]
        shares.append((1.0 / (total * (subjects * subj_devs)))[0:1])
    share = jnp.concatenate(shares, axis=1)

    back = {}
    for q in range(CHUNKS):
        span = pl.ds(q * rows, rows)
        for g in range(BLK_DEV):
            mapped = lax.dot_general(
                seen_x[g, span, :], last_maps[g], (((1,), (1,)), ((), ())),
                preferred_element_type=jnp.float32,
            )
            for a in range(SPAN):
                tiles[g, a] = mapped[:, a * BLOCK : (a + 1) * BLOCK]
        for w in range(WIN):
            cols = pl.ds((w % BLK_DEV) * BLOCK, BLOCK)
            both = sum(tiles[g, entry[g][w]] for g in range(BLK_DEV))
            if w // BLK_DEV == 1:
                own[span, cols] = both
            else:
                back_out[w // (2 * BLK_DEV), span, cols] = both.astype(LINK)
        for side in range(2):
            copy = pltpu.make_async_remote_copy(
                back_out.at[side, span], back_in.at[side, span],
                back_send.at[side, q], back_recv.at[side, q],
                device_id=sides[side], device_id_type=MESH,
            )
            copy.start()
            back[side, q] = copy

    parts, means = {}, {}

    def send_parts(q):
        span = pl.ds(q * rows, rows)
        for side in range(2):
            back[side, q].wait_recv()
        total = own[span] + back_in[0, span].astype(jnp.float32) + back_in[1, span].astype(jnp.float32)
        total = total * share
        own[span] = total
        part_out[span] = total.astype(LINK)
        for d in range(1, subj_devs):
            start = pl.multiple_of(q * rows + peers[d] * piece, piece)
            copy = pltpu.make_async_remote_copy(
                part_out.at[pl.ds(start, piece)], part_in.at[d - 1, pl.ds(q * piece, piece)],
                part_send.at[d - 1, q], part_recv.at[d - 1, q],
                device_id=(peers[d], me_c), device_id_type=MESH,
            )
            copy.start()
            parts[d, q] = copy

    def send_means(q):
        span = pl.ds(q * piece, piece)
        for d in range(1, subj_devs):
            parts[d, q].wait_recv()
        start = pl.multiple_of(q * rows + me_s * piece, piece)
        total = own[pl.ds(start, piece)]
        for d in range(1, subj_devs):
            total = total + part_in[d - 1, span].astype(jnp.float32)
        mean_out[span] = total.astype(LINK)
        here = gathered.at[pl.ds(start, piece)]
        copy = pltpu.make_async_copy(mean_out.at[span], here, mean_send.at[subj_devs - 1, q])
        copy.start()
        means[0, q] = copy
        for d in range(1, subj_devs):
            copy = pltpu.make_async_remote_copy(
                mean_out.at[span], here, mean_send.at[d - 1, q], mean_recv.at[d - 1, q],
                device_id=(peers[d], me_c), device_id_type=MESH,
            )
            copy.start()
            means[d, q] = copy

    for q in range(CHUNKS):
        send_parts(q)
        if q >= 1:
            send_means(q - 1)
    send_means(CHUNKS - 1)
    for copy in halo.values():
        copy.wait_send()
    for copy in (*back.values(), *parts.values()):
        copy.wait_send()
    for copy in means.values():
        copy.wait()


def body(series, template, lists):
    subjects, frames, own_width = series.shape
    subj_devs, cortex_devs = lax.axis_size("subj"), lax.axis_size("cortex")
    width = SPAN * BLOCK
    rows = frames // CHUNKS
    piece = rows // subj_devs
    bf16, f32, dma = jnp.bfloat16, jnp.float32, pltpu.SemaphoreType.DMA
    gathered = pl.pallas_call(
        functools.partial(kernel, subj_devs, cortex_devs),
        out_shape=jax.ShapeDtypeStruct((frames, own_width), LINK),
        in_specs=[
            pl.BlockSpec(memory_space=pltpu.SMEM),
            pl.BlockSpec(memory_space=pl.ANY),
            pl.BlockSpec(memory_space=pl.ANY),
        ],
        out_specs=pl.BlockSpec(memory_space=pl.ANY),
        scratch_shapes=[
            *[pltpu.VMEM((WIN, frames, BLOCK), bf16)] * subjects,
            pltpu.VMEM((WIN, frames, BLOCK), bf16),
            pltpu.VMEM((BLK_DEV, frames, subjects * width), bf16),
            pltpu.VMEM((BLK_DEV, width, frames), bf16),
            pltpu.VMEM((BLK_DEV, width, width), bf16),
            pltpu.VMEM((BLK_DEV, width, subjects * width), bf16),
            pltpu.VMEM((BLK_DEV, SPAN + 1, rows, BLOCK), f32),
            pltpu.VMEM((frames, own_width), f32),
            pltpu.VMEM((2, frames, own_width), LINK),
            pltpu.VMEM((2, frames, own_width), LINK),
            pltpu.VMEM((frames, own_width), LINK),
            pltpu.VMEM((subj_devs - 1, CHUNKS * piece, own_width), LINK),
            pltpu.VMEM((CHUNKS * piece, own_width), LINK),
            pltpu.VMEM((2, 8 * BLK_DEV, BLOCK), f32),
            pltpu.VMEM((2, 8 * BLK_DEV, BLOCK), f32),
            dma(((1 + subjects) * BLK_DEV,)),
            dma((1 + subjects, 2, BLK_DEV)),
            dma((1 + subjects, 2, BLK_DEV)),
            dma((2,)),
            dma((2,)),
            dma((2, CHUNKS)),
            dma((2, CHUNKS)),
            dma((subj_devs - 1, CHUNKS)),
            dma((subj_devs - 1, CHUNKS)),
            dma((subj_devs, CHUNKS)),
            dma((subj_devs - 1, CHUNKS)),
        ],
        compiler_params=pltpu.CompilerParams(
            collective_id=0, has_side_effects=True, vmem_limit_bytes=48 << 20
        ),
        name="searchlights",
    )(lists, series, template)
    return gathered.astype(f32)


def solution(mesh):
    in_specs = (P("subj", None, "cortex"), P(None, "cortex"), P("cortex", None))
    out_specs = P(None, "cortex")
    return jax.shard_map(body, mesh=mesh, in_specs=in_specs, out_specs=out_specs, check_vma=False)
```

```python
import functools

import jax
import jax.numpy as jnp
from jax import lax
from jax.experimental import pallas as pl
from jax.experimental.pallas import tpu as pltpu
from jax.sharding import PartitionSpec as P

BLOCK = 128
NS_STEPS = 8
BLK_DEV = 2
SPAN = 3
WIN = 3 * BLK_DEV
RIDGE_SHIFT = 0.1
NORM_EPSILON = 1e-06
CHUNKS = 2
RELAYS = 4
MESH = pl.DeviceIdType.MESH
LINK = jnp.bfloat16


def kernel(
    subj_devs, cortex_devs, lists_hbm, series, template, gathered, lists,
    win_x0, win_x1, win_p, seen_x, seen_pt, maps, gram, last_maps, tiles, own, back_out, back_in,
    part_out, part_in, mean_out, count_out, count_in,
    load_sem, halo_send, halo_recv, share_send, share_recv, near_send, near_recv, count_send, count_recv,
    back_send, back_recv, part_send, part_recv, mean_send, mean_recv,
):
    subjects, frames = series.shape[0], series.shape[1]
    width, edge = SPAN * BLOCK, (SPAN - 1) * BLOCK
    rows = frames // CHUNKS
    piece = rows // subj_devs
    me_s, me_c = lax.axis_index("subj"), lax.axis_index("cortex")
    left = (me_s, lax.rem(me_c + cortex_devs - 1, cortex_devs))
    right = (me_s, lax.rem(me_c + 1, cortex_devs))
    sides = (left, right)
    win_x = (win_x0, win_x1)
    peers = [lax.rem(me_s + d, subj_devs) for d in range(subj_devs)]

    barrier = pltpu.get_barrier_semaphore()
    for device in (*sides, *((p, me_c) for p in peers[1:])):
        pl.semaphore_signal(barrier, inc=1, device_id=device, device_id_type=MESH)

    loads = [(lists_hbm, lists)]
    for b in range(BLK_DEV):
        cols = pl.ds(b * BLOCK, BLOCK)
        loads.append((template.at[:, cols], win_p.at[BLK_DEV + b]))
        for s in range(subjects):
            loads.append((series.at[s, :, cols], win_x[s].at[BLK_DEV + b]))
    loads = [pltpu.make_async_copy(a, b, load_sem.at[i]) for i, (a, b) in enumerate(loads)]
    for copy in loads:
        copy.start()
    loads.pop(0).wait()

    first = (me_c - 1) * BLK_DEV
    place = [
        [jnp.clip(lists[g, a] - first, 0, WIN - 1) for a in range(SPAN)] for g in range(BLK_DEV)
    ]
    entry = [
        [
            jnp.where(p[0] == w, 0, jnp.where(p[1] == w, 1, jnp.where(p[2] == w, 2, SPAN)))
            for w in range(WIN)
        ]
        for p in place
    ]
    counts = []
    for w in range(WIN):
        c = sum(jnp.where(p == w, 1.0, 0.0) for q in place for p in q)
        counts.append(jnp.full((8, BLOCK), c, jnp.float32))
    for b in range(BLK_DEV):
        count_out[0, pl.ds(8 * b, 8)] = counts[b]
        count_out[1, pl.ds(8 * b, 8)] = counts[2 * BLK_DEV + b]
    for g in range(BLK_DEV):
        tiles[g, SPAN] = jnp.zeros(tiles.shape[2:], tiles.dtype)

    pl.semaphore_wait(barrier, 2 + subj_devs - 1)

    core = lax.rem(me_c, 2)
    near = (me_s, me_c + 1 - 2 * core)
    far = (me_s, lax.rem(me_c - 1 + 2 * core + cortex_devs, cortex_devs))
    turn = lax.rem(me_s, RELAYS)
    share_rows = frames // RELAYS
    mine = pl.ds(pl.multiple_of(turn * share_rows, share_rows), share_rows)
    far_spot = 2 * BLK_DEV * core
    halo, relays = {}, []
    for b in range(BLK_DEV):
        cols = pl.ds(b * BLOCK, BLOCK)
        copy = pltpu.make_async_remote_copy(
            template.at[mine, cols], win_p.at[2 * BLK_DEV - far_spot + b, mine],
            share_send.at[0, b], share_recv.at[0, b], device_id=far, device_id_type=MESH,
        )
        copy.start()
        relays.append(copy)
    for item in range(subjects):
        for side in range(2):
            for b in range(BLK_DEV):
                cols = pl.ds(b * BLOCK, BLOCK)
                spot = (2 * BLK_DEV if side == 0 else 0) + b
                copy = pltpu.make_async_remote_copy(
                    series.at[item, :, cols], win_x[item].at[spot],
                    halo_send.at[item, side, b], halo_recv.at[item, side, b],
                    device_id=sides[side], device_id_type=MESH,
                )
                copy.start()
                halo[item, side, b] = copy
        if item == 0:
            for b in range(BLK_DEV):
                cols = pl.ds(b * BLOCK, BLOCK)
                copy = pltpu.make_async_remote_copy(
                    template.at[:, cols], win_p.at[far_spot + b],
                    near_send.at[b], near_recv.at[b], device_id=near, device_id_type=MESH,
                )
                copy.start()
                halo[-1, 0, b] = copy
    tally = []
    for side in range(2):
        copy = pltpu.make_async_remote_copy(
            count_out.at[side], count_in.at[side], count_send.at[side], count_recv.at[side],
            device_id=sides[side], device_id_type=MESH,
        )
        copy.start()
        tally.append(copy)
    for copy in list(relays):
        copy.wait_recv()
    for d in range(1, RELAYS):
        peer = me_s - turn + lax.rem(turn + d, RELAYS)
        for b in range(BLK_DEV):
            part = win_p.at[far_spot + b, mine]
            copy = pltpu.make_async_remote_copy(
                part, part, share_send.at[d, b], share_recv.at[d, b],
                device_id=(peer, me_c), device_id_type=MESH,
            )
            copy.start()
            relays.append(copy)
    for copy in loads:
        copy.wait()

    def arrived(item):
        for side in range(2):
            for b in range(BLK_DEV):
                halo[item, side, b].wait_recv()

    on_diagonal = lax.broadcasted_iota(jnp.int32, (width, width), 0) == lax.broadcasted_iota(
        jnp.int32, (width, width), 1
    )
    for b in range(BLK_DEV):
        halo[-1, 0, b].wait_recv()
    for copy in relays[BLK_DEV:]:
        copy.wait_recv()
    for g in range(BLK_DEV):
        for a in range(SPAN):
            seen_pt[g, pl.ds(a * BLOCK, BLOCK), :] = win_p[place[g][a]].T
    for s in range(subjects):
        arrived(s)
        for g in range(BLK_DEV):
            for a in range(SPAN):
                seen_x[g, :, pl.ds((s * SPAN + a) * BLOCK, BLOCK)] = win_x[s][place[g][a]]
        for g in range(BLK_DEV):
            cross = lax.dot_general(
                seen_pt[g], seen_x[g, :, pl.ds(s * width, width)], (((1,), (0,)), ((), ())),
                preferred_element_type=jnp.float32,
            )
            cross = cross * (1.0 / frames) + jnp.where(on_diagonal, RIDGE_SHIFT, 0.0)
            scale = lax.rsqrt(jnp.sum(cross * cross, keepdims=True) + NORM_EPSILON)
            maps[g] = (cross * scale).astype(jnp.bfloat16)

        def step(_, carry):
            for g in range(BLK_DEV):
                gram[g, :, :edge] = lax.dot_general(
                    maps[g], maps[g, :edge], (((1,), (1,)), ((), ())),
                    preferred_element_type=jnp.float32,
                ).astype(jnp.bfloat16)
            for g in range(BLK_DEV):
                gram[g, edge:, edge:] = lax.dot_general(
                    maps[g, edge:], maps[g, edge:], (((1,), (1,)), ((), ())),
                    preferred_element_type=jnp.float32,
                ).astype(jnp.bfloat16)
                gram[g, :edge, edge:] = gram[g, edge:, :edge].T
            for g in range(BLK_DEV):
                product = lax.dot_general(
                    gram[g], maps[g], (((1,), (0,)), ((), ())), preferred_element_type=jnp.float32
                )
                maps[g] = (1.5 * maps[g].astype(jnp.float32) - 0.5 * product).astype(jnp.bfloat16)
            return carry

        lax.fori_loop(0, NS_STEPS, step, 0, unroll=2)
        for g in range(BLK_DEV):
            last_maps[g, :, pl.ds(s * width, width)] = maps[g]

    for copy in tally:
        copy.wait()
    shares = []
    for b in range(BLK_DEV):
        total = counts[BLK_DEV + b] + count_in[0, pl.ds(8 * b, 8)] + count_in[1, pl.ds(8 * b, 8)]
        shares.append((1.0 / (total * (subjects * subj_devs)))[0:1])
    share = jnp.concatenate(shares, axis=1)

    back = {}
    for q in range(CHUNKS):
        span = pl.ds(q * rows, rows)
        for g in range(BLK_DEV):
            mapped = lax.dot_general(
                seen_x[g, span, :], last_maps[g], (((1,), (1,)), ((), ())),
                preferred_element_type=jnp.float32,
            )
            for a in range(SPAN):
                tiles[g, a] = mapped[:, a * BLOCK : (a + 1) * BLOCK]
        for w in range(WIN):
            cols = pl.ds((w % BLK_DEV) * BLOCK, BLOCK)
            both = sum(tiles[g, entry[g][w]] for g in range(BLK_DEV))
            if w // BLK_DEV == 1:
                own[span, cols] = both
            else:
                back_out[w // (2 * BLK_DEV), span, cols] = both.astype(LINK)
        for side in range(2):
            copy = pltpu.make_async_remote_copy(
                back_out.at[side, span], back_in.at[side, span],
                back_send.at[side, q], back_recv.at[side, q],
                device_id=sides[side], device_id_type=MESH,
            )
            copy.start()
            back[side, q] = copy

    parts, means = {}, {}

    def send_parts(q):
        span = pl.ds(q * rows, rows)
        for side in range(2):
            back[side, q].wait_recv()
        total = own[span] + back_in[0, span].astype(jnp.float32) + back_in[1, span].astype(jnp.float32)
        total = total * share
        own[span] = total
        part_out[span] = total.astype(LINK)
        for d in range(1, subj_devs):
            start = pl.multiple_of(q * rows + peers[d] * piece, piece)
            copy = pltpu.make_async_remote_copy(
                part_out.at[pl.ds(start, piece)], part_in.at[d - 1, pl.ds(q * piece, piece)],
                part_send.at[d - 1, q], part_recv.at[d - 1, q],
                device_id=(peers[d], me_c), device_id_type=MESH,
            )
            copy.start()
            parts[d, q] = copy

    def send_means(q):
        span = pl.ds(q * piece, piece)
        for d in range(1, subj_devs):
            parts[d, q].wait_recv()
        start = pl.multiple_of(q * rows + me_s * piece, piece)
        total = own[pl.ds(start, piece)]
        for d in range(1, subj_devs):
            total = total + part_in[d - 1, span].astype(jnp.float32)
        mean_out[span] = total.astype(LINK)
        here = gathered.at[pl.ds(start, piece)]
        copy = pltpu.make_async_copy(mean_out.at[span], here, mean_send.at[subj_devs - 1, q])
        copy.start()
        means[0, q] = copy
        for d in range(1, subj_devs):
            copy = pltpu.make_async_remote_copy(
                mean_out.at[span], here, mean_send.at[d - 1, q], mean_recv.at[d - 1, q],
                device_id=(peers[d], me_c), device_id_type=MESH,
            )
            copy.start()
            means[d, q] = copy

    for q in range(CHUNKS):
        send_parts(q)
        if q >= 1:
            send_means(q - 1)
    send_means(CHUNKS - 1)
    for copy in (*halo.values(), *relays):
        copy.wait_send()
    for copy in (*back.values(), *parts.values()):
        copy.wait_send()
    for copy in means.values():
        copy.wait()


def body(series, template, lists):
    subjects, frames, own_width = series.shape
    subj_devs, cortex_devs = lax.axis_size("subj"), lax.axis_size("cortex")
    width = SPAN * BLOCK
    rows = frames // CHUNKS
    piece = rows // subj_devs
    bf16, f32, dma = jnp.bfloat16, jnp.float32, pltpu.SemaphoreType.DMA
    gathered = pl.pallas_call(
        functools.partial(kernel, subj_devs, cortex_devs),
        out_shape=jax.ShapeDtypeStruct((frames, own_width), LINK),
        in_specs=[
            pl.BlockSpec(memory_space=pltpu.HBM),
            pl.BlockSpec(memory_space=pltpu.HBM),
            pl.BlockSpec(memory_space=pltpu.HBM),
        ],
        out_specs=pl.BlockSpec(memory_space=pl.ANY),
        scratch_shapes=[
            pltpu.SMEM((BLK_DEV, SPAN), jnp.int32),
            *[pltpu.VMEM((WIN, frames, BLOCK), bf16)] * subjects,
            pltpu.VMEM((WIN, frames, BLOCK), bf16),
            pltpu.VMEM((BLK_DEV, frames, subjects * width), bf16),
            pltpu.VMEM((BLK_DEV, width, frames), bf16),
            pltpu.VMEM((BLK_DEV, width, width), bf16),
            pltpu.VMEM((BLK_DEV, width, width), bf16),
            pltpu.VMEM((BLK_DEV, width, subjects * width), bf16),
            pltpu.VMEM((BLK_DEV, SPAN + 1, rows, BLOCK), f32),
            pltpu.VMEM((frames, own_width), f32),
            pltpu.VMEM((2, frames, own_width), LINK),
            pltpu.VMEM((2, frames, own_width), LINK),
            pltpu.VMEM((frames, own_width), LINK),
            pltpu.VMEM((subj_devs - 1, CHUNKS * piece, own_width), LINK),
            pltpu.VMEM((CHUNKS * piece, own_width), LINK),
            pltpu.VMEM((2, 8 * BLK_DEV, BLOCK), f32),
            pltpu.VMEM((2, 8 * BLK_DEV, BLOCK), f32),
            dma(((1 + subjects) * BLK_DEV + 1,)),
            dma((subjects, 2, BLK_DEV)),
            dma((subjects, 2, BLK_DEV)),
            dma((RELAYS, BLK_DEV)),
            dma((RELAYS, BLK_DEV)),
            dma((BLK_DEV,)),
            dma((BLK_DEV,)),
            dma((2,)),
            dma((2,)),
            dma((2, CHUNKS)),
            dma((2, CHUNKS)),
            dma((subj_devs - 1, CHUNKS)),
            dma((subj_devs - 1, CHUNKS)),
            dma((subj_devs, CHUNKS)),
            dma((subj_devs - 1, CHUNKS)),
        ],
        compiler_params=pltpu.CompilerParams(
            collective_id=0, has_side_effects=True, vmem_limit_bytes=63 << 20
        ),
        name="searchlights",
    )(lists, series, template)
    return gathered.astype(f32)


def solution(mesh):
    in_specs = (P("subj", None, "cortex"), P(None, "cortex"), P("cortex", None))
    out_specs = P(None, "cortex")
    return jax.shard_map(body, mesh=mesh, in_specs=in_specs, out_specs=out_specs, check_vma=False)
```

```python
import functools

import jax
import jax.numpy as jnp
from jax import lax
from jax.experimental import pallas as pl
from jax.experimental.pallas import tpu as pltpu
from jax.sharding import PartitionSpec as P

BLOCK = 128
NS_STEPS = 8
BLK_DEV = 2
SPAN = 3
WIN = 3 * BLK_DEV
RIDGE_SHIFT = 0.1
NORM_EPSILON = 1e-06
CHUNKS = 4
RELAYS = 4
MESH = pl.DeviceIdType.MESH
LINK = jnp.bfloat16


def kernel(
    subj_devs, cortex_devs, lists_hbm, series, template, gathered, lists,
    win_x0, win_x1, win_p, seen_x, seen_pt, maps, gram, last_maps, spread, own, back_out, back_in,
    part_out, part_in, mean_out, count_out, count_in,
    ready_sem, load_sem, halo_send, halo_recv, share_send, share_recv, near_send, near_recv, count_send, count_recv,
    back_send, back_recv, part_send, part_recv, mean_send, mean_recv,
):
    subjects, frames = series.shape[0], series.shape[1]
    width, edge = SPAN * BLOCK, (SPAN - 1) * BLOCK
    rows = frames // CHUNKS
    piece = rows // subj_devs
    me_s, me_c = lax.axis_index("subj"), lax.axis_index("cortex")
    left = (me_s, lax.rem(me_c + cortex_devs - 1, cortex_devs))
    right = (me_s, lax.rem(me_c + 1, cortex_devs))
    sides = (left, right)
    win_x = (win_x0, win_x1)
    peers = [lax.rem(me_s + d, subj_devs) for d in range(subj_devs)]

    turn = lax.rem(me_s, RELAYS)
    mates = [me_s - turn + lax.rem(turn + d, RELAYS) for d in range(1, RELAYS)]
    across = peers[RELAYS]
    greeted = [*sides, *((p, me_c) for p in mates), (across, me_c)]
    barrier = pltpu.get_barrier_semaphore()
    for device in greeted:
        pl.semaphore_signal(barrier, inc=1, device_id=device, device_id_type=MESH)

    loads = [(lists_hbm, lists)]
    for b in range(BLK_DEV):
        cols = pl.ds(b * BLOCK, BLOCK)
        loads.append((template.at[:, cols], win_p.at[BLK_DEV + b]))
        for s in range(subjects):
            loads.append((series.at[s, :, cols], win_x[s].at[BLK_DEV + b]))
    loads = [pltpu.make_async_copy(a, b, load_sem.at[i]) for i, (a, b) in enumerate(loads)]
    for copy in loads:
        copy.start()
    loads.pop(0).wait()

    first = (me_c - 1) * BLK_DEV
    place = [
        [jnp.clip(lists[g, a] - first, 0, WIN - 1) for a in range(SPAN)] for g in range(BLK_DEV)
    ]
    entry = [
        [
            jnp.where(p[0] == w, 0, jnp.where(p[1] == w, 1, jnp.where(p[2] == w, 2, SPAN)))
            for w in range(WIN)
        ]
        for p in place
    ]
    counts = []
    for w in range(WIN):
        c = sum(jnp.where(p == w, 1.0, 0.0) for q in place for p in q)
        counts.append(jnp.full((8, BLOCK), c, jnp.float32))
    for b in range(BLK_DEV):
        count_out[0, pl.ds(8 * b, 8)] = counts[b]
        count_out[1, pl.ds(8 * b, 8)] = counts[2 * BLK_DEV + b]
    for g in range(BLK_DEV):
        last_maps[g, SPAN] = jnp.zeros(last_maps.shape[2:], last_maps.dtype)

    pl.semaphore_wait(barrier, len(greeted))
    pl.semaphore_signal(ready_sem, inc=1, device_id=(across, me_c), device_id_type=MESH)

    core = lax.rem(me_c, 2)
    near = (me_s, me_c + 1 - 2 * core)
    far = (me_s, lax.rem(me_c - 1 + 2 * core + cortex_devs, cortex_devs))
    share_rows = frames // RELAYS
    mine = pl.ds(pl.multiple_of(turn * share_rows, share_rows), share_rows)
    far_spot = 2 * BLK_DEV * core
    halo, relays = {}, []
    for b in range(BLK_DEV):
        cols = pl.ds(b * BLOCK, BLOCK)
        copy = pltpu.make_async_remote_copy(
            template.at[mine, cols], win_p.at[2 * BLK_DEV - far_spot + b, mine],
            share_send.at[0, b], share_recv.at[0, b], device_id=far, device_id_type=MESH,
        )
        copy.start()
        relays.append(copy)
    def send_series(item):
        for side in range(2):
            for b in range(BLK_DEV):
                cols = pl.ds(b * BLOCK, BLOCK)
                spot = (2 * BLK_DEV if side == 0 else 0) + b
                copy = pltpu.make_async_remote_copy(
                    series.at[item, :, cols], win_x[item].at[spot],
                    halo_send.at[item, side, b], halo_recv.at[item, side, b],
                    device_id=sides[side], device_id_type=MESH,
                )
                copy.start()
                halo[item, side, b] = copy

    def series_left(item):
        for side in range(2):
            for b in range(BLK_DEV):
                halo[item, side, b].wait_send()

    send_series(0)
    nears = []
    for b in range(BLK_DEV):
        cols = pl.ds(b * BLOCK, BLOCK)
        copy = pltpu.make_async_remote_copy(
            template.at[:, cols], win_p.at[far_spot + b],
            near_send.at[b], near_recv.at[b], device_id=near, device_id_type=MESH,
        )
        copy.start()
        nears.append(copy)
    tally = []
    for side in range(2):
        copy = pltpu.make_async_remote_copy(
            count_out.at[side], count_in.at[side], count_send.at[side], count_recv.at[side],
            device_id=sides[side], device_id_type=MESH,
        )
        copy.start()
        tally.append(copy)
    for copy in list(relays):
        copy.wait_recv()
    for d in range(1, RELAYS):
        for b in range(BLK_DEV):
            part = win_p.at[far_spot + b, mine]
            copy = pltpu.make_async_remote_copy(
                part, part, share_send.at[d, b], share_recv.at[d, b],
                device_id=(mates[d - 1], me_c), device_id_type=MESH,
            )
            copy.start()
            relays.append(copy)
    for copy in loads:
        copy.wait()
    for item in range(1, subjects):
        series_left(item - 1)
        send_series(item)

    def arrived(item):
        for side in range(2):
            for b in range(BLK_DEV):
                halo[item, side, b].wait_recv()

    on_diagonal = lax.broadcasted_iota(jnp.int32, (width, width), 0) == lax.broadcasted_iota(
        jnp.int32, (width, width), 1
    )
    for copy in (*nears, *relays[BLK_DEV:]):
        copy.wait_recv()
    for g in range(BLK_DEV):
        for a in range(SPAN):
            seen_pt[g, pl.ds(a * BLOCK, BLOCK), :] = win_p[place[g][a]].T
    for s in range(subjects):
        arrived(s)
        for g in range(BLK_DEV):
            for a in range(SPAN):
                seen_x[:, pl.ds(((g * subjects + s) * SPAN + a) * BLOCK, BLOCK)] = win_x[s][place[g][a]]
        for g in range(BLK_DEV):
            cross = lax.dot_general(
                seen_pt[g], seen_x[:, pl.ds((g * subjects + s) * width, width)], (((1,), (0,)), ((), ())),
                preferred_element_type=jnp.float32,
            )
            cross = cross * (1.0 / frames) + jnp.where(on_diagonal, RIDGE_SHIFT, 0.0)
            scale = lax.rsqrt(jnp.sum(cross * cross, keepdims=True) + NORM_EPSILON)
            maps[g] = (cross * scale).astype(jnp.bfloat16)

        def step(_, carry):
            for g in range(BLK_DEV):
                gram[g, :, :edge] = lax.dot_general(
                    maps[g], maps[g, :edge], (((1,), (1,)), ((), ())),
                    preferred_element_type=jnp.float32,
                ).astype(jnp.bfloat16)
            for g in range(BLK_DEV):
                gram[g, edge:, edge:] = lax.dot_general(
                    maps[g, edge:], maps[g, edge:], (((1,), (1,)), ((), ())),
                    preferred_element_type=jnp.float32,
                ).astype(jnp.bfloat16)
                gram[g, :edge, edge:] = gram[g, edge:, :edge].T
            for g in range(BLK_DEV):
                product = lax.dot_general(
                    gram[g], maps[g], (((1,), (0,)), ((), ())), preferred_element_type=jnp.float32
                )
                maps[g] = (1.5 * maps[g].astype(jnp.float32) - 0.5 * product).astype(jnp.bfloat16)
            return carry

        lax.fori_loop(0, NS_STEPS, step, 0, unroll=2)
        for g in range(BLK_DEV):
            for a in range(SPAN):
                last_maps[g, a, :, pl.ds(s * width, width)] = maps[g, a * BLOCK : (a + 1) * BLOCK]

    for copy in tally:
        copy.wait()
    shares = []
    for b in range(BLK_DEV):
        total = counts[BLK_DEV + b] + count_in[0, pl.ds(8 * b, 8)] + count_in[1, pl.ds(8 * b, 8)]
        shares.append((1.0 / (total * (subjects * subj_devs)))[0:1])
    share = jnp.concatenate(shares, axis=1)

    for w in range(WIN):
        for g in range(BLK_DEV):
            spread[
                w // BLK_DEV,
                pl.ds((w % BLK_DEV) * BLOCK, BLOCK),
                pl.ds(g * subjects * width, subjects * width),
            ] = last_maps[g, entry[g][w]]

    def mapped(third, span):
        return lax.dot_general(
            seen_x[span, :], spread[third], (((1,), (1,)), ((), ())),
            preferred_element_type=jnp.float32,
        )

    back = {}

    def map_sides(q):
        span = pl.ds(q * rows, rows)
        for side in range(2):
            back_out[side, span] = mapped(2 * side, span).astype(LINK)

    def send_back(q):
        span = pl.ds(q * rows, rows)
        for side in range(2):
            copy = pltpu.make_async_remote_copy(
                back_out.at[side, span], back_in.at[side, span],
                back_send.at[side, q], back_recv.at[side, q],
                device_id=sides[side], device_id_type=MESH,
            )
            copy.start()
            back[side, q] = copy

    parts, means = {}, {}

    def send_parts(q):
        span = pl.ds(q * rows, rows)
        for side in range(2):
            back[side, q].wait_recv()
        total = own[span] + back_in[0, span].astype(jnp.float32) + back_in[1, span].astype(jnp.float32)
        total = total * share
        own[span] = total
        part_out[span] = total.astype(LINK)
        for d in range(1, subj_devs):
            start = pl.multiple_of(q * rows + peers[d] * piece, piece)
            copy = pltpu.make_async_remote_copy(
                part_out.at[pl.ds(start, piece)], part_in.at[d - 1, pl.ds(q * piece, piece)],
                part_send.at[d - 1, q], part_recv.at[d - 1, q],
                device_id=(peers[d], me_c), device_id_type=MESH,
            )
            copy.start()
            parts[d, q] = copy

    def send_means(q):
        span = pl.ds(q * piece, piece)
        for d in range(1, subj_devs):
            parts[d, q].wait_recv()
        start = pl.multiple_of(q * rows + me_s * piece, piece)
        total = own[pl.ds(start, piece)]
        for d in range(1, subj_devs):
            total = total + part_in[d - 1, span].astype(jnp.float32)
        mean_out[span] = total.astype(LINK)
        here = gathered.at[pl.ds(start, piece)]
        copy = pltpu.make_async_copy(mean_out.at[span], here, mean_send.at[subj_devs - 1, q])
        copy.start()
        means[0, q] = copy
        for d in range(1, subj_devs):
            copy = pltpu.make_async_remote_copy(
                mean_out.at[span], here, mean_send.at[d - 1, q], mean_recv.at[d - 1, q],
                device_id=(peers[d], me_c), device_id_type=MESH,
            )
            copy.start()
            means[d, q] = copy

    map_sides(0)
    send_back(0)
    pl.semaphore_wait(ready_sem, 1)
    for q in range(CHUNKS):
        span = pl.ds(q * rows, rows)
        own[span] = mapped(1, span)
        if q < CHUNKS - 1:
            map_sides(q + 1)
        for side in range(2):
            back[side, q].wait_send()
        if q < CHUNKS - 1:
            send_back(q + 1)
        send_parts(q)
    for q in range(CHUNKS):
        send_means(q)
    series_left(subjects - 1)
    for copy in (*nears, *relays, *parts.values()):
        copy.wait_send()
    for copy in means.values():
        copy.wait()


def body(series, template, lists):
    subjects, frames, own_width = series.shape
    subj_devs, cortex_devs = lax.axis_size("subj"), lax.axis_size("cortex")
    width = SPAN * BLOCK
    rows = frames // CHUNKS
    piece = rows // subj_devs
    bf16, f32, dma = jnp.bfloat16, jnp.float32, pltpu.SemaphoreType.DMA
    gathered = pl.pallas_call(
        functools.partial(kernel, subj_devs, cortex_devs),
        out_shape=jax.ShapeDtypeStruct((frames, own_width), LINK),
        in_specs=[
            pl.BlockSpec(memory_space=pltpu.HBM),
            pl.BlockSpec(memory_space=pltpu.HBM),
            pl.BlockSpec(memory_space=pltpu.HBM),
        ],
        out_specs=pl.BlockSpec(memory_space=pl.ANY),
        scratch_shapes=[
            pltpu.SMEM((BLK_DEV, SPAN), jnp.int32),
            *[pltpu.VMEM((WIN, frames, BLOCK), bf16)] * subjects,
            pltpu.VMEM((WIN, frames, BLOCK), bf16),
            pltpu.VMEM((frames, BLK_DEV * subjects * width), bf16),
            pltpu.VMEM((BLK_DEV, width, frames), bf16),
            pltpu.VMEM((BLK_DEV, width, width), bf16),
            pltpu.VMEM((BLK_DEV, width, width), bf16),
            pltpu.VMEM((BLK_DEV, SPAN + 1, BLOCK, subjects * width), bf16),
            pltpu.VMEM((SPAN, BLK_DEV * BLOCK, BLK_DEV * subjects * width), bf16),
            pltpu.VMEM((frames, own_width), f32),
            pltpu.VMEM((2, frames, own_width), LINK),
            pltpu.VMEM((2, frames, own_width), LINK),
            pltpu.VMEM((frames, own_width), LINK),
            pltpu.VMEM((subj_devs - 1, CHUNKS * piece, own_width), LINK),
            pltpu.VMEM((CHUNKS * piece, own_width), LINK),
            pltpu.VMEM((2, 8 * BLK_DEV, BLOCK), f32),
            pltpu.VMEM((2, 8 * BLK_DEV, BLOCK), f32),
            pltpu.SemaphoreType.REGULAR,
            dma(((1 + subjects) * BLK_DEV + 1,)),
            dma((subjects, 2, BLK_DEV)),
            dma((subjects, 2, BLK_DEV)),
            dma((RELAYS, BLK_DEV)),
            dma((RELAYS, BLK_DEV)),
            dma((BLK_DEV,)),
            dma((BLK_DEV,)),
            dma((2,)),
            dma((2,)),
            dma((2, CHUNKS)),
            dma((2, CHUNKS)),
            dma((subj_devs - 1, CHUNKS)),
            dma((subj_devs - 1, CHUNKS)),
            dma((subj_devs, CHUNKS)),
            dma((subj_devs - 1, CHUNKS)),
        ],
        compiler_params=pltpu.CompilerParams(
            collective_id=0, has_side_effects=True, vmem_limit_bytes=40 << 20
        ),
        name="searchlights",
    )(*(pltpu.with_memory_space_constraint(a, pltpu.HBM) for a in (lists, series, template)))
    return gathered.astype(f32)


def solution(mesh):
    in_specs = (P("subj", None, "cortex"), P(None, "cortex"), P("cortex", None))
    out_specs = P(None, "cortex")
    return jax.shard_map(body, mesh=mesh, in_specs=in_specs, out_specs=out_specs, check_vma=False)
```

```python
import functools

import jax
import jax.numpy as jnp
from jax import lax
from jax.experimental import pallas as pl
from jax.experimental.pallas import tpu as pltpu
from jax.sharding import PartitionSpec as P

BLOCK = 128
NS_STEPS = 8
BLK_DEV = 2
SPAN = 3
WIN = 3 * BLK_DEV
RIDGE_SHIFT = 0.1
NORM_EPSILON = 1e-06
CHUNKS = 2
RELAYS = 4
MESH = pl.DeviceIdType.MESH
LINK = jnp.bfloat16


def kernel(
    subj_devs, cortex_devs, lists_hbm, series, template, gathered, lists,
    win_x0, win_x1, win_p, seen_x, seen_pt, maps, gram, last_maps, spread, own, back_out, back_in,
    part_out, part_in, mean_out, count_out, count_in,
    ready_sem, load_sem, halo_send, halo_recv, share_send, share_recv, near_send, near_recv, count_send, count_recv,
    back_send, back_recv, part_send, part_recv, mean_send, mean_recv,
):
    subjects, frames = series.shape[0], series.shape[1]
    width, edge = SPAN * BLOCK, (SPAN - 1) * BLOCK
    rows = frames // CHUNKS
    piece = rows // subj_devs
    me_s, me_c = lax.axis_index("subj"), lax.axis_index("cortex")
    left = (me_s, lax.rem(me_c + cortex_devs - 1, cortex_devs))
    right = (me_s, lax.rem(me_c + 1, cortex_devs))
    sides = (left, right)
    win_x = (win_x0, win_x1)
    turn = lax.rem(me_s, RELAYS)
    half = me_s - turn
    other = subj_devs - RELAYS - half
    mates = [half + lax.rem(turn + d, RELAYS) for d in range(1, RELAYS)]
    across = other + turn
    beyond = [other + lax.rem(turn + d, RELAYS) for d in range(1, RELAYS)]
    peers = [me_s, beyond[1], beyond[0], beyond[2], mates[1], across, mates[0], mates[2]]

    greeted = [*sides, *((p, me_c) for p in mates), (across, me_c)]
    barrier = pltpu.get_barrier_semaphore()
    for device in greeted:
        pl.semaphore_signal(barrier, inc=1, device_id=device, device_id_type=MESH)

    loads = [(lists_hbm, lists)]
    for b in range(BLK_DEV):
        cols = pl.ds(b * BLOCK, BLOCK)
        loads.append((template.at[:, cols], win_p.at[BLK_DEV + b]))
        for s in range(subjects):
            loads.append((series.at[s, :, cols], win_x[s].at[BLK_DEV + b]))
    loads = [pltpu.make_async_copy(a, b, load_sem.at[i]) for i, (a, b) in enumerate(loads)]
    for copy in loads:
        copy.start()
    loads.pop(0).wait()

    first = (me_c - 1) * BLK_DEV
    place = [
        [jnp.clip(lists[g, a] - first, 0, WIN - 1) for a in range(SPAN)] for g in range(BLK_DEV)
    ]
    entry = [
        [
            jnp.where(p[0] == w, 0, jnp.where(p[1] == w, 1, jnp.where(p[2] == w, 2, SPAN)))
            for w in range(WIN)
        ]
        for p in place
    ]
    counts = []
    for w in range(WIN):
        c = sum(jnp.where(p == w, 1.0, 0.0) for q in place for p in q)
        counts.append(jnp.full((8, BLOCK), c, jnp.float32))
    for b in range(BLK_DEV):
        count_out[0, pl.ds(8 * b, 8)] = counts[b]
        count_out[1, pl.ds(8 * b, 8)] = counts[2 * BLK_DEV + b]
    for g in range(BLK_DEV):
        last_maps[g, SPAN] = jnp.zeros(last_maps.shape[2:], last_maps.dtype)

    pl.semaphore_wait(barrier, len(greeted))
    pl.semaphore_signal(ready_sem, inc=1, device_id=(across, me_c), device_id_type=MESH)

    core = lax.rem(me_c, 2)
    near = (me_s, me_c + 1 - 2 * core)
    far = (me_s, lax.rem(me_c - 1 + 2 * core + cortex_devs, cortex_devs))
    share_rows = frames // RELAYS
    mine = pl.ds(pl.multiple_of(turn * share_rows, share_rows), share_rows)
    far_spot = 2 * BLK_DEV * core
    halo, relays = {}, []
    for b in range(BLK_DEV):
        cols = pl.ds(b * BLOCK, BLOCK)
        copy = pltpu.make_async_remote_copy(
            template.at[mine, cols], win_p.at[2 * BLK_DEV - far_spot + b, mine],
            share_send.at[0, b], share_recv.at[0, b], device_id=far, device_id_type=MESH,
        )
        copy.start()
        relays.append(copy)
    def send_series(item):
        for side in range(2):
            for b in range(BLK_DEV):
                cols = pl.ds(b * BLOCK, BLOCK)
                spot = (2 * BLK_DEV if side == 0 else 0) + b
                copy = pltpu.make_async_remote_copy(
                    series.at[item, :, cols], win_x[item].at[spot],
                    halo_send.at[item, side, b], halo_recv.at[item, side, b],
                    device_id=sides[side], device_id_type=MESH,
                )
                copy.start()
                halo[item, side, b] = copy

    def series_left(item):
        for side in range(2):
            for b in range(BLK_DEV):
                halo[item, side, b].wait_send()

    for copy in relays:
        copy.wait_send()
    send_series(0)
    nears = []
    for b in range(BLK_DEV):
        cols = pl.ds(b * BLOCK, BLOCK)
        copy = pltpu.make_async_remote_copy(
            template.at[:, cols], win_p.at[far_spot + b],
            near_send.at[b], near_recv.at[b], device_id=near, device_id_type=MESH,
        )
        copy.start()
        nears.append(copy)
    tally = []
    for side in range(2):
        copy = pltpu.make_async_remote_copy(
            count_out.at[side], count_in.at[side], count_send.at[side], count_recv.at[side],
            device_id=sides[side], device_id_type=MESH,
        )
        copy.start()
        tally.append(copy)
    for copy in list(relays):
        copy.wait_recv()
    for d in range(1, RELAYS):
        for b in range(BLK_DEV):
            part = win_p.at[far_spot + b, mine]
            copy = pltpu.make_async_remote_copy(
                part, part, share_send.at[d, b], share_recv.at[d, b],
                device_id=(mates[d - 1], me_c), device_id_type=MESH,
            )
            copy.start()
            relays.append(copy)
    for copy in loads:
        copy.wait()
    for item in range(1, subjects):
        series_left(item - 1)
        send_series(item)

    def arrived(item):
        for side in range(2):
            for b in range(BLK_DEV):
                halo[item, side, b].wait_recv()

    on_diagonal = lax.broadcasted_iota(jnp.int32, (width, width), 0) == lax.broadcasted_iota(
        jnp.int32, (width, width), 1
    )
    for copy in (*nears, *relays[BLK_DEV:]):
        copy.wait_recv()
    for g in range(BLK_DEV):
        for a in range(SPAN):
            seen_pt[g, pl.ds(a * BLOCK, BLOCK), :] = win_p[place[g][a]].T
    for s in range(subjects):
        arrived(s)
        for g in range(BLK_DEV):
            for a in range(SPAN):
                seen_x[:, pl.ds(((g * subjects + s) * SPAN + a) * BLOCK, BLOCK)] = win_x[s][place[g][a]]
        for g in range(BLK_DEV):
            cross = lax.dot_general(
                seen_pt[g], seen_x[:, pl.ds((g * subjects + s) * width, width)], (((1,), (0,)), ((), ())),
                preferred_element_type=jnp.float32,
            )
            cross = cross * (1.0 / frames) + jnp.where(on_diagonal, RIDGE_SHIFT, 0.0)
            scale = lax.rsqrt(jnp.sum(cross * cross, keepdims=True) + NORM_EPSILON)
            maps[g] = (cross * scale).astype(jnp.bfloat16)

        def step(_, carry):
            for g in range(BLK_DEV):
                gram[g, :, :edge] = lax.dot_general(
                    maps[g], maps[g, :edge], (((1,), (1,)), ((), ())),
                    preferred_element_type=jnp.float32,
                ).astype(jnp.bfloat16)
            for g in range(BLK_DEV):
                gram[g, edge:, edge:] = lax.dot_general(
                    maps[g, edge:], maps[g, edge:], (((1,), (1,)), ((), ())),
                    preferred_element_type=jnp.float32,
                ).astype(jnp.bfloat16)
                gram[g, :edge, edge:] = gram[g, edge:, :edge].T
            for g in range(BLK_DEV):
                product = lax.dot_general(
                    gram[g], maps[g], (((1,), (0,)), ((), ())), preferred_element_type=jnp.float32
                )
                maps[g] = (1.5 * maps[g].astype(jnp.float32) - 0.5 * product).astype(jnp.bfloat16)
            return carry

        lax.fori_loop(0, NS_STEPS, step, 0, unroll=4)
        for g in range(BLK_DEV):
            for a in range(SPAN):
                last_maps[g, a, :, pl.ds(s * width, width)] = maps[g, a * BLOCK : (a + 1) * BLOCK]

    for copy in tally:
        copy.wait()
    shares = []
    for b in range(BLK_DEV):
        total = counts[BLK_DEV + b] + count_in[0, pl.ds(8 * b, 8)] + count_in[1, pl.ds(8 * b, 8)]
        shares.append((1.0 / (total * (subjects * subj_devs)))[0:1])
    share = jnp.concatenate(shares, axis=1)

    for w in range(WIN):
        for g in range(BLK_DEV):
            spread[
                w // BLK_DEV,
                pl.ds((w % BLK_DEV) * BLOCK, BLOCK),
                pl.ds(g * subjects * width, subjects * width),
            ] = last_maps[g, entry[g][w]]

    def mapped(third, span):
        return lax.dot_general(
            seen_x[span, :], spread[third], (((1,), (1,)), ((), ())),
            preferred_element_type=jnp.float32,
        )

    back = {}

    def map_sides(q):
        span = pl.ds(q * rows, rows)
        for side in range(2):
            back_out[side, span] = mapped(2 * side, span).astype(LINK)

    def send_back(q):
        span = pl.ds(q * rows, rows)
        for side in range(2):
            copy = pltpu.make_async_remote_copy(
                back_out.at[side, span], back_in.at[side, span],
                back_send.at[side, q], back_recv.at[side, q],
                device_id=sides[side], device_id_type=MESH,
            )
            copy.start()
            back[side, q] = copy

    parts, means = {}, {}

    def send_parts(q):
        span = pl.ds(q * rows, rows)
        for side in range(2):
            back[side, q].wait_recv()
        total = own[span] + back_in[0, span].astype(jnp.float32) + back_in[1, span].astype(jnp.float32)
        total = total * share
        own[span] = total
        part_out[span] = total.astype(LINK)
        for d in range(1, subj_devs):
            start = pl.multiple_of(q * rows + peers[d] * piece, piece)
            copy = pltpu.make_async_remote_copy(
                part_out.at[pl.ds(start, piece)], part_in.at[d - 1, pl.ds(q * piece, piece)],
                part_send.at[d - 1, q], part_recv.at[d - 1, q],
                device_id=(peers[d], me_c), device_id_type=MESH,
            )
            copy.start()
            parts[d, q] = copy

    def send_means(q):
        span = pl.ds(q * piece, piece)
        for d in range(1, subj_devs):
            parts[d, q].wait_recv()
        start = pl.multiple_of(q * rows + me_s * piece, piece)
        total = own[pl.ds(start, piece)]
        for d in range(1, subj_devs):
            total = total + part_in[d - 1, span].astype(jnp.float32)
        mean_out[span] = total.astype(LINK)
        here = gathered.at[pl.ds(start, piece)]
        copy = pltpu.make_async_copy(mean_out.at[span], here, mean_send.at[subj_devs - 1, q])
        copy.start()
        means[0, q] = copy
        for d in range(1, subj_devs):
            copy = pltpu.make_async_remote_copy(
                mean_out.at[span], here, mean_send.at[d - 1, q], mean_recv.at[d - 1, q],
                device_id=(peers[d], me_c), device_id_type=MESH,
            )
            copy.start()
            means[d, q] = copy

    map_sides(0)
    send_back(0)
    pl.semaphore_wait(ready_sem, 1)
    for q in range(CHUNKS):
        span = pl.ds(q * rows, rows)
        own[span] = mapped(1, span)
        if q < CHUNKS - 1:
            map_sides(q + 1)
        for side in range(2):
            back[side, q].wait_send()
        if q < CHUNKS - 1:
            send_back(q + 1)
        send_parts(q)
    for q in range(CHUNKS):
        send_means(q)
    series_left(subjects - 1)
    for copy in (*nears, *relays[BLK_DEV:], *parts.values()):
        copy.wait_send()
    for copy in means.values():
        copy.wait()


def body(series, template, lists):
    subjects, frames, own_width = series.shape
    subj_devs, cortex_devs = lax.axis_size("subj"), lax.axis_size("cortex")
    width = SPAN * BLOCK
    rows = frames // CHUNKS
    piece = rows // subj_devs
    bf16, f32, dma = jnp.bfloat16, jnp.float32, pltpu.SemaphoreType.DMA
    gathered = pl.pallas_call(
        functools.partial(kernel, subj_devs, cortex_devs),
        out_shape=jax.ShapeDtypeStruct((frames, own_width), LINK),
        in_specs=[
            pl.BlockSpec(memory_space=pltpu.HBM),
            pl.BlockSpec(memory_space=pltpu.HBM),
            pl.BlockSpec(memory_space=pltpu.HBM),
        ],
        out_specs=pl.BlockSpec(memory_space=pl.ANY),
        scratch_shapes=[
            pltpu.SMEM((BLK_DEV, SPAN), jnp.int32),
            *[pltpu.VMEM((WIN, frames, BLOCK), bf16)] * subjects,
            pltpu.VMEM((WIN, frames, BLOCK), bf16),
            pltpu.VMEM((frames, BLK_DEV * subjects * width), bf16),
            pltpu.VMEM((BLK_DEV, width, frames), bf16),
            pltpu.VMEM((BLK_DEV, width, width), bf16),
            pltpu.VMEM((BLK_DEV, width, width), bf16),
            pltpu.VMEM((BLK_DEV, SPAN + 1, BLOCK, subjects * width), bf16),
            pltpu.VMEM((SPAN, BLK_DEV * BLOCK, BLK_DEV * subjects * width), bf16),
            pltpu.VMEM((frames, own_width), f32),
            pltpu.VMEM((2, frames, own_width), LINK),
            pltpu.VMEM((2, frames, own_width), LINK),
            pltpu.VMEM((frames, own_width), LINK),
            pltpu.VMEM((subj_devs - 1, CHUNKS * piece, own_width), LINK),
            pltpu.VMEM((CHUNKS * piece, own_width), LINK),
            pltpu.VMEM((2, 8 * BLK_DEV, BLOCK), f32),
            pltpu.VMEM((2, 8 * BLK_DEV, BLOCK), f32),
            pltpu.SemaphoreType.REGULAR,
            dma(((1 + subjects) * BLK_DEV + 1,)),
            dma((subjects, 2, BLK_DEV)),
            dma((subjects, 2, BLK_DEV)),
            dma((RELAYS, BLK_DEV)),
            dma((RELAYS, BLK_DEV)),
            dma((BLK_DEV,)),
            dma((BLK_DEV,)),
            dma((2,)),
            dma((2,)),
            dma((2, CHUNKS)),
            dma((2, CHUNKS)),
            dma((subj_devs - 1, CHUNKS)),
            dma((subj_devs - 1, CHUNKS)),
            dma((subj_devs, CHUNKS)),
            dma((subj_devs - 1, CHUNKS)),
        ],
        compiler_params=pltpu.CompilerParams(
            collective_id=0, has_side_effects=True, vmem_limit_bytes=40 << 20
        ),
        name="searchlights",
    )(*(pltpu.with_memory_space_constraint(a, pltpu.HBM) for a in (lists, series, template)))
    return gathered.astype(f32)


def solution(mesh):
    in_specs = (P("subj", None, "cortex"), P(None, "cortex"), P("cortex", None))
    out_specs = P(None, "cortex")
    return jax.shard_map(body, mesh=mesh, in_specs=in_specs, out_specs=out_specs, check_vma=False)
```

```python
import functools

import jax
import jax.numpy as jnp
from jax import lax
from jax.experimental import pallas as pl
from jax.experimental.pallas import tpu as pltpu
from jax.sharding import PartitionSpec as P

BLOCK = 128
NS_STEPS = 8
BLK_DEV = 2
SPAN = 3
WIN = 3 * BLK_DEV
RIDGE_SHIFT = 0.1
NORM_EPSILON = 1e-06
SHARES = (3, 3, 2)
CHUNKS = len(SHARES)
RELAYS = 4
MESH = pl.DeviceIdType.MESH
LINK = jnp.bfloat16


def kernel(
    subj_devs, cortex_devs, lists_hbm, series, template, gathered, lists,
    win_x0, win_x1, win_p, seen_x, seen_pt, maps, gram, last_maps, spread, own, back_out, back_in,
    part_out, part_in, mean_out, count_out, count_in,
    ready_sem, load_sem, halo_send, halo_recv, share_send, share_recv, near_send, near_recv, count_send, count_recv,
    back_send, back_recv, part_send, part_recv, mean_send, mean_recv,
):
    subjects, frames = series.shape[0], series.shape[1]
    width, edge = SPAN * BLOCK, (SPAN - 1) * BLOCK
    ends = [sum(SHARES[:q]) * frames // sum(SHARES) for q in range(CHUNKS + 1)]
    chunks = [pl.ds(a, b - a) for a, b in zip(ends, ends[1:])]
    slots = [pl.ds(a // subj_devs, (b - a) // subj_devs) for a, b in zip(ends, ends[1:])]

    def piece(q, device):
        rows = slots[q].size
        return pl.ds(pl.multiple_of(ends[q] + device * rows, 16), rows)

    me_s, me_c = lax.axis_index("subj"), lax.axis_index("cortex")
    left = (me_s, lax.rem(me_c + cortex_devs - 1, cortex_devs))
    right = (me_s, lax.rem(me_c + 1, cortex_devs))
    sides = (left, right)
    win_x = (win_x0, win_x1)
    turn = lax.rem(me_s, RELAYS)
    half = me_s - turn
    other = subj_devs - RELAYS - half
    mates = [half + lax.rem(turn + d, RELAYS) for d in range(1, RELAYS)]
    across = other + turn
    beyond = [other + lax.rem(turn + d, RELAYS) for d in range(1, RELAYS)]
    peers = [me_s, beyond[1], beyond[0], beyond[2], mates[1], across, mates[0], mates[2]]

    greeted = [*sides, *((p, me_c) for p in mates), (across, me_c)]
    barrier = pltpu.get_barrier_semaphore()
    for device in greeted:
        pl.semaphore_signal(barrier, inc=1, device_id=device, device_id_type=MESH)

    loads = [(lists_hbm, lists)]
    for b in range(BLK_DEV):
        cols = pl.ds(b * BLOCK, BLOCK)
        loads.append((template.at[:, cols], win_p.at[BLK_DEV + b]))
        for s in range(subjects):
            loads.append((series.at[s, :, cols], win_x[s].at[BLK_DEV + b]))
    loads = [pltpu.make_async_copy(a, b, load_sem.at[i]) for i, (a, b) in enumerate(loads)]
    for copy in loads:
        copy.start()
    loads.pop(0).wait()

    first = (me_c - 1) * BLK_DEV
    place = [
        [jnp.clip(lists[g, a] - first, 0, WIN - 1) for a in range(SPAN)] for g in range(BLK_DEV)
    ]
    entry = [
        [
            jnp.where(p[0] == w, 0, jnp.where(p[1] == w, 1, jnp.where(p[2] == w, 2, SPAN)))
            for w in range(WIN)
        ]
        for p in place
    ]
    counts = []
    for w in range(WIN):
        c = sum(jnp.where(p == w, 1.0, 0.0) for q in place for p in q)
        counts.append(jnp.full((8, BLOCK), c, jnp.float32))
    for b in range(BLK_DEV):
        count_out[0, pl.ds(8 * b, 8)] = counts[b]
        count_out[1, pl.ds(8 * b, 8)] = counts[2 * BLK_DEV + b]
    for g in range(BLK_DEV):
        last_maps[g, SPAN] = jnp.zeros(last_maps.shape[2:], last_maps.dtype)

    pl.semaphore_wait(barrier, len(greeted))
    pl.semaphore_signal(ready_sem, inc=1, device_id=(across, me_c), device_id_type=MESH)

    core = lax.rem(me_c, 2)
    near = (me_s, me_c + 1 - 2 * core)
    far = (me_s, lax.rem(me_c - 1 + 2 * core + cortex_devs, cortex_devs))
    share_rows = frames // RELAYS
    mine = pl.ds(pl.multiple_of(turn * share_rows, share_rows), share_rows)
    far_spot = 2 * BLK_DEV * core
    halo, relays = {}, []
    for b in range(BLK_DEV):
        cols = pl.ds(b * BLOCK, BLOCK)
        copy = pltpu.make_async_remote_copy(
            template.at[mine, cols], win_p.at[2 * BLK_DEV - far_spot + b, mine],
            share_send.at[0, b], share_recv.at[0, b], device_id=far, device_id_type=MESH,
        )
        copy.start()
        relays.append(copy)
    def send_series(item):
        for side in range(2):
            for b in range(BLK_DEV):
                cols = pl.ds(b * BLOCK, BLOCK)
                spot = (2 * BLK_DEV if side == 0 else 0) + b
                copy = pltpu.make_async_remote_copy(
                    series.at[item, :, cols], win_x[item].at[spot],
                    halo_send.at[item, side, b], halo_recv.at[item, side, b],
                    device_id=sides[side], device_id_type=MESH,
                )
                copy.start()
                halo[item, side, b] = copy

    def series_left(item):
        for side in range(2):
            for b in range(BLK_DEV):
                halo[item, side, b].wait_send()

    for copy in relays:
        copy.wait_send()
    send_series(0)
    nears = []
    for b in range(BLK_DEV):
        cols = pl.ds(b * BLOCK, BLOCK)
        copy = pltpu.make_async_remote_copy(
            template.at[:, cols], win_p.at[far_spot + b],
            near_send.at[b], near_recv.at[b], device_id=near, device_id_type=MESH,
        )
        copy.start()
        nears.append(copy)
    tally = []
    for side in range(2):
        copy = pltpu.make_async_remote_copy(
            count_out.at[side], count_in.at[side], count_send.at[side], count_recv.at[side],
            device_id=sides[side], device_id_type=MESH,
        )
        copy.start()
        tally.append(copy)
    for copy in list(relays):
        copy.wait_recv()
    for d in (2, 1, 3):
        for b in range(BLK_DEV):
            part = win_p.at[far_spot + b, mine]
            copy = pltpu.make_async_remote_copy(
                part, part, share_send.at[d, b], share_recv.at[d, b],
                device_id=(mates[d - 1], me_c), device_id_type=MESH,
            )
            copy.start()
            relays.append(copy)
    for copy in loads:
        copy.wait()
    for item in range(1, subjects):
        series_left(item - 1)
        send_series(item)

    def arrived(item):
        for side in range(2):
            for b in range(BLK_DEV):
                halo[item, side, b].wait_recv()

    on_diagonal = lax.broadcasted_iota(jnp.int32, (width, width), 0) == lax.broadcasted_iota(
        jnp.int32, (width, width), 1
    )
    for copy in (*nears, *relays[BLK_DEV:]):
        copy.wait_recv()
    for g in range(BLK_DEV):
        for a in range(SPAN):
            seen_pt[g, pl.ds(a * BLOCK, BLOCK), :] = win_p[place[g][a]].T
    for s in range(subjects):
        arrived(s)
        for g in range(BLK_DEV):
            for a in range(SPAN):
                seen_x[:, pl.ds(((g * subjects + s) * SPAN + a) * BLOCK, BLOCK)] = win_x[s][place[g][a]]
        for g in range(BLK_DEV):
            cross = lax.dot_general(
                seen_pt[g], seen_x[:, pl.ds((g * subjects + s) * width, width)], (((1,), (0,)), ((), ())),
                preferred_element_type=jnp.float32,
            )
            cross = cross * (1.0 / frames) + jnp.where(on_diagonal, RIDGE_SHIFT, 0.0)
            scale = lax.rsqrt(jnp.sum(cross * cross, keepdims=True) + NORM_EPSILON)
            maps[g] = (cross * scale).astype(jnp.bfloat16)

        def step(_, carry):
            for g in range(BLK_DEV):
                gram[g, :, :edge] = lax.dot_general(
                    maps[g], maps[g, :edge], (((1,), (1,)), ((), ())),
                    preferred_element_type=jnp.float32,
                ).astype(jnp.bfloat16)
            for g in range(BLK_DEV):
                gram[g, edge:, edge:] = lax.dot_general(
                    maps[g, edge:], maps[g, edge:], (((1,), (1,)), ((), ())),
                    preferred_element_type=jnp.float32,
                ).astype(jnp.bfloat16)
                gram[g, :edge, edge:] = gram[g, edge:, :edge].T
            for g in range(BLK_DEV):
                product = lax.dot_general(
                    gram[g], maps[g], (((1,), (0,)), ((), ())), preferred_element_type=jnp.float32
                )
                maps[g] = (1.5 * maps[g].astype(jnp.float32) - 0.5 * product).astype(jnp.bfloat16)
            return carry

        lax.fori_loop(0, NS_STEPS, step, 0, unroll=4)
        for g in range(BLK_DEV):
            for a in range(SPAN):
                last_maps[g, a, :, pl.ds(s * width, width)] = maps[g, a * BLOCK : (a + 1) * BLOCK]

    for copy in tally:
        copy.wait()
    shares = []
    for b in range(BLK_DEV):
        total = counts[BLK_DEV + b] + count_in[0, pl.ds(8 * b, 8)] + count_in[1, pl.ds(8 * b, 8)]
        shares.append((1.0 / (total * (subjects * subj_devs)))[0:1])
    share = jnp.concatenate(shares, axis=1)

    for w in range(WIN):
        for g in range(BLK_DEV):
            spread[
                w // BLK_DEV,
                pl.ds((w % BLK_DEV) * BLOCK, BLOCK),
                pl.ds(g * subjects * width, subjects * width),
            ] = last_maps[g, entry[g][w]]

    def mapped(third, span):
        return lax.dot_general(
            seen_x[span, :], spread[third], (((1,), (1,)), ((), ())),
            preferred_element_type=jnp.float32,
        )

    back = {}

    def map_sides(q):
        span = chunks[q]
        for side in range(2):
            back_out[side, span] = mapped(2 * side, span).astype(LINK)

    def send_back(q):
        span = chunks[q]
        for side in range(2):
            copy = pltpu.make_async_remote_copy(
                back_out.at[side, span], back_in.at[side, span],
                back_send.at[side, q], back_recv.at[side, q],
                device_id=sides[side], device_id_type=MESH,
            )
            copy.start()
            back[side, q] = copy

    parts, means = {}, {}

    def send_parts(q):
        span = chunks[q]
        for side in range(2):
            back[side, q].wait_recv()
        total = own[span] + back_in[0, span].astype(jnp.float32) + back_in[1, span].astype(jnp.float32)
        total = total * share
        own[span] = total
        part_out[span] = total.astype(LINK)
        for d in range(1, subj_devs):
            copy = pltpu.make_async_remote_copy(
                part_out.at[piece(q, peers[d])], part_in.at[d - 1, slots[q]],
                part_send.at[d - 1, q], part_recv.at[d - 1, q],
                device_id=(peers[d], me_c), device_id_type=MESH,
            )
            copy.start()
            parts[d, q] = copy

    def send_means(q):
        span = slots[q]
        for d in range(1, subj_devs):
            parts[d, q].wait_recv()
        total = own[piece(q, me_s)]
        for d in range(1, subj_devs):
            total = total + part_in[d - 1, span].astype(jnp.float32)
        mean_out[span] = total.astype(LINK)
        here = gathered.at[piece(q, me_s)]
        copy = pltpu.make_async_copy(mean_out.at[span], here, mean_send.at[subj_devs - 1, q])
        copy.start()
        means[0, q] = copy
        for d in range(1, subj_devs):
            copy = pltpu.make_async_remote_copy(
                mean_out.at[span], here, mean_send.at[d - 1, q], mean_recv.at[d - 1, q],
                device_id=(peers[d], me_c), device_id_type=MESH,
            )
            copy.start()
            means[d, q] = copy

    map_sides(0)
    send_back(0)
    map_sides(1)
    send_back(1)
    pl.semaphore_wait(ready_sem, 1)
    for q in range(CHUNKS):
        span = chunks[q]
        own[span] = mapped(1, span)
        if q < CHUNKS - 2:
            map_sides(q + 2)
        for side in range(2):
            back[side, q].wait_send()
        if q < CHUNKS - 2:
            send_back(q + 2)
        send_parts(q)
    for q in range(CHUNKS):
        send_means(q)
    series_left(subjects - 1)
    for copy in (*nears, *relays[BLK_DEV:], *parts.values()):
        copy.wait_send()
    for copy in means.values():
        copy.wait()


def body(series, template, lists):
    subjects, frames, own_width = series.shape
    subj_devs, cortex_devs = lax.axis_size("subj"), lax.axis_size("cortex")
    width = SPAN * BLOCK
    bf16, f32, dma = jnp.bfloat16, jnp.float32, pltpu.SemaphoreType.DMA
    gathered = pl.pallas_call(
        functools.partial(kernel, subj_devs, cortex_devs),
        out_shape=jax.ShapeDtypeStruct((frames, own_width), LINK),
        in_specs=[
            pl.BlockSpec(memory_space=pltpu.HBM),
            pl.BlockSpec(memory_space=pltpu.HBM),
            pl.BlockSpec(memory_space=pltpu.HBM),
        ],
        out_specs=pl.BlockSpec(memory_space=pl.ANY),
        scratch_shapes=[
            pltpu.SMEM((BLK_DEV, SPAN), jnp.int32),
            *[pltpu.VMEM((WIN, frames, BLOCK), bf16)] * subjects,
            pltpu.VMEM((WIN, frames, BLOCK), bf16),
            pltpu.VMEM((frames, BLK_DEV * subjects * width), bf16),
            pltpu.VMEM((BLK_DEV, width, frames), bf16),
            pltpu.VMEM((BLK_DEV, width, width), bf16),
            pltpu.VMEM((BLK_DEV, width, width), bf16),
            pltpu.VMEM((BLK_DEV, SPAN + 1, BLOCK, subjects * width), bf16),
            pltpu.VMEM((SPAN, BLK_DEV * BLOCK, BLK_DEV * subjects * width), bf16),
            pltpu.VMEM((frames, own_width), f32),
            pltpu.VMEM((2, frames, own_width), LINK),
            pltpu.VMEM((2, frames, own_width), LINK),
            pltpu.VMEM((frames, own_width), LINK),
            pltpu.VMEM((subj_devs - 1, frames // subj_devs, own_width), LINK),
            pltpu.VMEM((frames // subj_devs, own_width), LINK),
            pltpu.VMEM((2, 8 * BLK_DEV, BLOCK), f32),
            pltpu.VMEM((2, 8 * BLK_DEV, BLOCK), f32),
            pltpu.SemaphoreType.REGULAR,
            dma(((1 + subjects) * BLK_DEV + 1,)),
            dma((subjects, 2, BLK_DEV)),
            dma((subjects, 2, BLK_DEV)),
            dma((RELAYS, BLK_DEV)),
            dma((RELAYS, BLK_DEV)),
            dma((BLK_DEV,)),
            dma((BLK_DEV,)),
            dma((2,)),
            dma((2,)),
            dma((2, CHUNKS)),
            dma((2, CHUNKS)),
            dma((subj_devs - 1, CHUNKS)),
            dma((subj_devs - 1, CHUNKS)),
            dma((subj_devs, CHUNKS)),
            dma((subj_devs - 1, CHUNKS)),
        ],
        compiler_params=pltpu.CompilerParams(
            collective_id=0, has_side_effects=True, vmem_limit_bytes=40 << 20
        ),
        name="searchlights",
    )(*(pltpu.with_memory_space_constraint(a, pltpu.HBM) for a in (lists, series, template)))
    return gathered.astype(f32)


def solution(mesh):
    in_specs = (P("subj", None, "cortex"), P(None, "cortex"), P("cortex", None))
    out_specs = P(None, "cortex")
    return jax.shard_map(body, mesh=mesh, in_specs=in_specs, out_specs=out_specs, check_vma=False)
```

```python
import functools

import jax
import jax.numpy as jnp
from jax import lax
from jax.experimental import pallas as pl
from jax.experimental.pallas import tpu as pltpu
from jax.sharding import PartitionSpec as P

BLOCK = 128
NS_STEPS = 8
BLK_DEV = 2
SPAN = 3
WIN = 3 * BLK_DEV
RIDGE_SHIFT = 0.1
NORM_EPSILON = 1e-06
SHARES = (3, 3, 2)
CHUNKS = len(SHARES)
RELAYS = 4
MESH = pl.DeviceIdType.MESH
LINK = jnp.bfloat16


def kernel(
    subj_devs, cortex_devs, lists_hbm, series, template, gathered, lists,
    win_x0, win_x1, win_p, seen_x, seen_pt, maps, gram, last_maps, spread, own, back_out, back_in,
    part_out, part_in, mean_out, count_out, count_in,
    ready_sem, load_sem, halo_send, halo_recv, share_send, share_recv, near_send, near_recv, count_send, count_recv,
    back_send, back_recv, part_send, part_recv, mean_send, mean_recv,
):
    subjects, frames = series.shape[0], series.shape[1]
    width, edge = SPAN * BLOCK, (SPAN - 1) * BLOCK
    ends = [sum(SHARES[:q]) * frames // sum(SHARES) for q in range(CHUNKS + 1)]
    chunks = [pl.ds(a, b - a) for a, b in zip(ends, ends[1:])]
    slots = [pl.ds(a // subj_devs, (b - a) // subj_devs) for a, b in zip(ends, ends[1:])]

    def piece(q, device):
        rows = slots[q].size
        return pl.ds(pl.multiple_of(ends[q] + device * rows, 16), rows)

    me_s, me_c = lax.axis_index("subj"), lax.axis_index("cortex")
    left = (me_s, lax.rem(me_c + cortex_devs - 1, cortex_devs))
    right = (me_s, lax.rem(me_c + 1, cortex_devs))
    sides = (left, right)
    win_x = (win_x0, win_x1)
    turn = lax.rem(me_s, RELAYS)
    half = me_s - turn
    other = subj_devs - RELAYS - half
    mates = [half + lax.rem(turn + d, RELAYS) for d in range(1, RELAYS)]
    across = other + turn
    beyond = [other + lax.rem(turn + d, RELAYS) for d in range(1, RELAYS)]
    peers = [me_s, beyond[1], beyond[0], beyond[2], mates[1], across, mates[0], mates[2]]

    greeted = [*sides, *((p, me_c) for p in mates), (across, me_c)]
    barrier = pltpu.get_barrier_semaphore()
    for device in greeted:
        pl.semaphore_signal(barrier, inc=1, device_id=device, device_id_type=MESH)

    loads = [(lists_hbm, lists)]
    for b in range(BLK_DEV):
        cols = pl.ds(b * BLOCK, BLOCK)
        loads.append((template.at[:, cols], win_p.at[BLK_DEV + b]))
        for s in range(subjects):
            loads.append((series.at[s, :, cols], win_x[s].at[BLK_DEV + b]))
    loads = [pltpu.make_async_copy(a, b, load_sem.at[i]) for i, (a, b) in enumerate(loads)]
    for copy in loads:
        copy.start()
    loads.pop(0).wait()

    first = (me_c - 1) * BLK_DEV
    place = [
        [jnp.clip(lists[g, a] - first, 0, WIN - 1) for a in range(SPAN)] for g in range(BLK_DEV)
    ]
    entry = [
        [
            jnp.where(p[0] == w, 0, jnp.where(p[1] == w, 1, jnp.where(p[2] == w, 2, SPAN)))
            for w in range(WIN)
        ]
        for p in place
    ]
    counts = []
    for w in range(WIN):
        c = sum(jnp.where(p == w, 1.0, 0.0) for q in place for p in q)
        counts.append(jnp.full((8, BLOCK), c, jnp.float32))
    for b in range(BLK_DEV):
        count_out[0, pl.ds(8 * b, 8)] = counts[b]
        count_out[1, pl.ds(8 * b, 8)] = counts[2 * BLK_DEV + b]
    for g in range(BLK_DEV):
        last_maps[g, SPAN] = jnp.zeros(last_maps.shape[2:], last_maps.dtype)

    pl.semaphore_wait(barrier, len(greeted))
    pl.semaphore_signal(ready_sem, inc=1, device_id=(across, me_c), device_id_type=MESH)

    core = lax.rem(me_c, 2)
    near = (me_s, me_c + 1 - 2 * core)
    far = (me_s, lax.rem(me_c - 1 + 2 * core + cortex_devs, cortex_devs))
    share_rows = frames // RELAYS
    mine = pl.ds(pl.multiple_of(turn * share_rows, share_rows), share_rows)
    far_spot = 2 * BLK_DEV * core
    halo, relays = {}, []
    for b in range(BLK_DEV):
        cols = pl.ds(b * BLOCK, BLOCK)
        copy = pltpu.make_async_remote_copy(
            template.at[mine, cols], win_p.at[2 * BLK_DEV - far_spot + b, mine],
            share_send.at[0, b], share_recv.at[0, b], device_id=far, device_id_type=MESH,
        )
        copy.start()
        relays.append(copy)
    def send_series(item):
        for side in range(2):
            for b in range(BLK_DEV):
                cols = pl.ds(b * BLOCK, BLOCK)
                spot = (2 * BLK_DEV if side == 0 else 0) + b
                copy = pltpu.make_async_remote_copy(
                    series.at[item, :, cols], win_x[item].at[spot],
                    halo_send.at[item, side, b], halo_recv.at[item, side, b],
                    device_id=sides[side], device_id_type=MESH,
                )
                copy.start()
                halo[item, side, b] = copy

    def series_left(item):
        for side in range(2):
            for b in range(BLK_DEV):
                halo[item, side, b].wait_send()

    for copy in relays:
        copy.wait_send()
    send_series(0)
    nears = []
    for b in range(BLK_DEV):
        cols = pl.ds(b * BLOCK, BLOCK)
        copy = pltpu.make_async_remote_copy(
            template.at[:, cols], win_p.at[far_spot + b],
            near_send.at[b], near_recv.at[b], device_id=near, device_id_type=MESH,
        )
        copy.start()
        nears.append(copy)
    tally = []
    for side in range(2):
        copy = pltpu.make_async_remote_copy(
            count_out.at[side], count_in.at[side], count_send.at[side], count_recv.at[side],
            device_id=sides[side], device_id_type=MESH,
        )
        copy.start()
        tally.append(copy)
    for copy in list(relays):
        copy.wait_recv()
    for d in (2, 1, 3):
        for b in range(BLK_DEV):
            part = win_p.at[far_spot + b, mine]
            copy = pltpu.make_async_remote_copy(
                part, part, share_send.at[d, b], share_recv.at[d, b],
                device_id=(mates[d - 1], me_c), device_id_type=MESH,
            )
            copy.start()
            relays.append(copy)
    for copy in loads:
        copy.wait()
    for item in range(1, subjects):
        series_left(item - 1)
        send_series(item)

    def arrived(item):
        for side in range(2):
            for b in range(BLK_DEV):
                halo[item, side, b].wait_recv()

    on_diagonal = lax.broadcasted_iota(jnp.int32, (width, width), 0) == lax.broadcasted_iota(
        jnp.int32, (width, width), 1
    )
    for copy in (*nears, *relays[BLK_DEV:]):
        copy.wait_recv()
    for g in range(BLK_DEV):
        for a in range(SPAN):
            seen_pt[g, pl.ds(a * BLOCK, BLOCK), :] = win_p[place[g][a]].T
    for s in range(subjects):
        arrived(s)
        for g in range(BLK_DEV):
            for a in range(SPAN):
                seen_x[:, pl.ds(((g * subjects + s) * SPAN + a) * BLOCK, BLOCK)] = win_x[s][place[g][a]]
        for g in range(BLK_DEV):
            cross = lax.dot_general(
                seen_pt[g], seen_x[:, pl.ds((g * subjects + s) * width, width)], (((1,), (0,)), ((), ())),
                preferred_element_type=jnp.float32,
            )
            cross = cross * (1.0 / frames) + jnp.where(on_diagonal, RIDGE_SHIFT, 0.0)
            scale = lax.rsqrt(jnp.sum(cross * cross, keepdims=True) + NORM_EPSILON)
            maps[g] = (cross * scale).astype(jnp.bfloat16)

        def step(_, carry):
            for g in range(BLK_DEV):
                gram[g, :, :edge] = lax.dot_general(
                    maps[g], maps[g, :edge], (((1,), (1,)), ((), ())),
                    preferred_element_type=jnp.float32,
                ).astype(jnp.bfloat16)
            for g in range(BLK_DEV):
                gram[g, edge:, edge:] = lax.dot_general(
                    maps[g, edge:], maps[g, edge:], (((1,), (1,)), ((), ())),
                    preferred_element_type=jnp.float32,
                ).astype(jnp.bfloat16)
                gram[g, :edge, edge:] = gram[g, edge:, :edge].T
            for g in range(BLK_DEV):
                product = lax.dot_general(
                    gram[g], maps[g], (((1,), (0,)), ((), ())), preferred_element_type=jnp.float32
                )
                maps[g] = (1.5 * maps[g].astype(jnp.float32) - 0.5 * product).astype(jnp.bfloat16)
            return carry

        lax.fori_loop(0, NS_STEPS, step, 0, unroll=4)
        for g in range(BLK_DEV):
            for a in range(SPAN):
                last_maps[g, a, :, pl.ds(s * width, width)] = maps[g, a * BLOCK : (a + 1) * BLOCK]

    for copy in tally:
        copy.wait()
    shares = []
    for b in range(BLK_DEV):
        total = counts[BLK_DEV + b] + count_in[0, pl.ds(8 * b, 8)] + count_in[1, pl.ds(8 * b, 8)]
        shares.append((1.0 / (total * (subjects * subj_devs)))[0:1])
    share = jnp.concatenate(shares, axis=1)

    def gather_maps(third):
        for w in range(BLK_DEV):
            for g in range(BLK_DEV):
                spread[
                    third, pl.ds(w * BLOCK, BLOCK), pl.ds(g * subjects * width, subjects * width)
                ] = last_maps[g, entry[g][third * BLK_DEV + w]]

    gather_maps(0)
    gather_maps(2)

    def mapped(third, span):
        return lax.dot_general(
            seen_x[span, :], spread[third], (((1,), (1,)), ((), ())),
            preferred_element_type=jnp.float32,
        )

    back = {}

    def map_sides(q):
        span = chunks[q]
        for side in range(2):
            back_out[side, span] = mapped(2 * side, span).astype(LINK)

    def send_back(q):
        span = chunks[q]
        for side in range(2):
            copy = pltpu.make_async_remote_copy(
                back_out.at[side, span], back_in.at[side, span],
                back_send.at[side, q], back_recv.at[side, q],
                device_id=sides[side], device_id_type=MESH,
            )
            copy.start()
            back[side, q] = copy

    parts, means = {}, {}

    def send_parts(q):
        span = chunks[q]
        for side in range(2):
            back[side, q].wait_recv()
        total = own[span] + back_in[0, span].astype(jnp.float32) + back_in[1, span].astype(jnp.float32)
        total = total * share
        own[span] = total
        part_out[span] = total.astype(LINK)
        for d in range(1, subj_devs):
            copy = pltpu.make_async_remote_copy(
                part_out.at[piece(q, peers[d])], part_in.at[d - 1, slots[q]],
                part_send.at[d - 1, q], part_recv.at[d - 1, q],
                device_id=(peers[d], me_c), device_id_type=MESH,
            )
            copy.start()
            parts[d, q] = copy

    def send_means(q):
        span = slots[q]
        for d in range(1, subj_devs):
            parts[d, q].wait_recv()
        total = own[piece(q, me_s)]
        for d in range(1, subj_devs):
            total = total + part_in[d - 1, span].astype(jnp.float32)
        mean_out[span] = total.astype(LINK)
        here = gathered.at[piece(q, me_s)]
        copy = pltpu.make_async_copy(mean_out.at[span], here, mean_send.at[subj_devs - 1, q])
        copy.start()
        means[0, q] = copy
        for d in range(1, subj_devs):
            copy = pltpu.make_async_remote_copy(
                mean_out.at[span], here, mean_send.at[d - 1, q], mean_recv.at[d - 1, q],
                device_id=(peers[d], me_c), device_id_type=MESH,
            )
            copy.start()
            means[d, q] = copy

    map_sides(0)
    send_back(0)
    map_sides(1)
    send_back(1)
    gather_maps(1)
    pl.semaphore_wait(ready_sem, 1)
    for q in range(CHUNKS):
        span = chunks[q]
        own[span] = mapped(1, span)
        if q < CHUNKS - 2:
            map_sides(q + 2)
        for side in range(2):
            back[side, q].wait_send()
        if q < CHUNKS - 2:
            send_back(q + 2)
        send_parts(q)
    for q in range(CHUNKS):
        send_means(q)
    series_left(subjects - 1)
    for copy in (*nears, *relays[BLK_DEV:], *parts.values()):
        copy.wait_send()
    for copy in means.values():
        copy.wait()


def body(series, template, lists):
    subjects, frames, own_width = series.shape
    subj_devs, cortex_devs = lax.axis_size("subj"), lax.axis_size("cortex")
    width = SPAN * BLOCK
    bf16, f32, dma = jnp.bfloat16, jnp.float32, pltpu.SemaphoreType.DMA
    gathered = pl.pallas_call(
        functools.partial(kernel, subj_devs, cortex_devs),
        out_shape=jax.ShapeDtypeStruct((frames, own_width), LINK),
        in_specs=[
            pl.BlockSpec(memory_space=pltpu.HBM),
            pl.BlockSpec(memory_space=pltpu.HBM),
            pl.BlockSpec(memory_space=pltpu.HBM),
        ],
        out_specs=pl.BlockSpec(memory_space=pl.ANY),
        scratch_shapes=[
            pltpu.SMEM((BLK_DEV, SPAN), jnp.int32),
            *[pltpu.VMEM((WIN, frames, BLOCK), bf16)] * subjects,
            pltpu.VMEM((WIN, frames, BLOCK), bf16),
            pltpu.VMEM((frames, BLK_DEV * subjects * width), bf16),
            pltpu.VMEM((BLK_DEV, width, frames), bf16),
            pltpu.VMEM((BLK_DEV, width, width), bf16),
            pltpu.VMEM((BLK_DEV, width, width), bf16),
            pltpu.VMEM((BLK_DEV, SPAN + 1, BLOCK, subjects * width), bf16),
            pltpu.VMEM((SPAN, BLK_DEV * BLOCK, BLK_DEV * subjects * width), bf16),
            pltpu.VMEM((frames, own_width), f32),
            pltpu.VMEM((2, frames, own_width), LINK),
            pltpu.VMEM((2, frames, own_width), LINK),
            pltpu.VMEM((frames, own_width), LINK),
            pltpu.VMEM((subj_devs - 1, frames // subj_devs, own_width), LINK),
            pltpu.VMEM((frames // subj_devs, own_width), LINK),
            pltpu.VMEM((2, 8 * BLK_DEV, BLOCK), f32),
            pltpu.VMEM((2, 8 * BLK_DEV, BLOCK), f32),
            pltpu.SemaphoreType.REGULAR,
            dma(((1 + subjects) * BLK_DEV + 1,)),
            dma((subjects, 2, BLK_DEV)),
            dma((subjects, 2, BLK_DEV)),
            dma((RELAYS, BLK_DEV)),
            dma((RELAYS, BLK_DEV)),
            dma((BLK_DEV,)),
            dma((BLK_DEV,)),
            dma((2,)),
            dma((2,)),
            dma((2, CHUNKS)),
            dma((2, CHUNKS)),
            dma((subj_devs - 1, CHUNKS)),
            dma((subj_devs - 1, CHUNKS)),
            dma((subj_devs, CHUNKS)),
            dma((subj_devs - 1, CHUNKS)),
        ],
        compiler_params=pltpu.CompilerParams(
            collective_id=0, has_side_effects=True, vmem_limit_bytes=40 << 20
        ),
        name="searchlights",
    )(*(pltpu.with_memory_space_constraint(a, pltpu.HBM) for a in (lists, series, template)))
    return gathered.astype(f32)


def solution(mesh):
    in_specs = (P("subj", None, "cortex"), P(None, "cortex"), P("cortex", None))
    out_specs = P(None, "cortex")
    return jax.shard_map(body, mesh=mesh, in_specs=in_specs, out_specs=out_specs, check_vma=False)
```
